32 devices in a mesh: stn: 16 (over z, y, core), pol: 2 (over x).
Axes of the slice: x: 2, y: 2, z: 4, core: 2. Of those that a mesh axis runs over, the one named last changes fastest.
Arguments:
- voltages: bfloat16 [64, 2, 2, 132992], P('stn', 'pol'), may hold values from -6 to 6, as said below
- delay_table: int32 [64], P('stn'), may hold values from 0 to 128
- channel_map: int32 [256], replicated, may hold values from 0 to 255, each once
- row_assign: int32 [32], replicated, may hold values from 0 to 31, each once
Outputs:
- bandpass: float32 [256, 128], P(('stn', 'pol'))
- lags: bfloat16 [32, 2, 256, 4, 128], P(('stn', 'pol'))
- delays: float32 [32, 4, 128], P(('stn', 'pol'))
The draws below stay inside these ranges and needn't reach their ends.
Inputs may be any that keep to these rules, and one draw needn't show every extreme that they name: `voltages`: A station's two polarizations and its real and imaginary parts are noisy copies of common signals with station-dependent time shifts. `channel_map`: each channel appears in exactly one slot. `row_assign`: each row block appears in exactly one slot.
All inputs are finite; a program needn't handle non-finite values.
Results may differ from the reference program's by a relative error of at most 0.0059.
Values may be sent and summed in bfloat16 or wider, within the bound.
A program may use at most 128 MiB of HBM per device.

```python
import math
import jax
import jax.numpy as jnp
from jax import lax

CHANNELS = 256
TAPS = 8
SPECTRA = 512
MAXD = 128
STATIONS = 64
INPUTS = 128
BLOCKS = 32
ROWB = 4
SAMPLES = 132992


def draw_voltages(key, part):
    key_common = jax.random.fold_in(key, 11)
    key_offset = jax.random.fold_in(key, 12)
    key_noise = jax.random.fold_in(key, 13)
    common = jax.random.normal(key_common, (2, 2, SAMPLES + MAXD), jnp.float32)
    offsets = jax.random.randint(key_offset, (STATIONS,), 0, MAXD + 1)
    noise_part = jax.random.normal(key_noise, (STATIONS, 2, 2, SAMPLES), jnp.float32)

    def shifted_copy(start_sample):
        return lax.dynamic_slice_in_dim(common, start_sample, SAMPLES, 2)
    shifted = jax.vmap(shifted_copy)(offsets)
    station_gain = jnp.ones((STATIONS, 2, 1, 1), jnp.float32)
    values = 0.8 * station_gain * shifted + 0.6 * noise_part
    return jnp.clip(values, -6.0, 6.0).astype(jnp.bfloat16)


def plant(result, stream_key, least, top_value):
    dims = result.shape
    place = [jax.random.randint(jax.random.fold_in(stream_key, axis), (), 0, dims[axis]) for axis in range(len(dims))]
    result = result.at[tuple(place)].set(least)
    longest = dims.index(max(dims))
    place[longest] = (place[longest] + 1) % dims[longest]
    return result.at[tuple(place)].set(top_value)


def setup_inputs(seed: int = 0) -> dict:
    seeds = jax.random.split(jax.random.key(seed), 5)
    voltages = draw_voltages(jax.random.fold_in(seeds[4], 71), 0)
    delay_table = plant(jax.random.randint(seeds[1], (STATIONS,), 0, MAXD + 1), jax.random.fold_in(seeds[1], 1), 0, MAXD).astype(jnp.int32)
    channel_map = jax.random.permutation(seeds[2], CHANNELS).astype(jnp.int32)
    row_assign = jax.random.permutation(seeds[3], BLOCKS).astype(jnp.int32)
    return {"voltages": voltages, "delay_table": delay_table, "channel_map": channel_map, "row_assign": row_assign}


def prototype():
    tap_total = TAPS * CHANNELS
    sample_index = jnp.arange(tap_total, dtype=jnp.float32)
    taper_values = 0.5 - 0.5 * jnp.cos(2.0 * math.pi * (sample_index + 0.5) / tap_total)
    offset = (sample_index - (tap_total - 1) / 2.0) / CHANNELS
    values = jnp.sin(math.pi * offset) / (math.pi * offset) * taper_values
    values = values * jnp.sqrt(CHANNELS / jnp.sum(values * values))
    return values.reshape(TAPS, CHANNELS)

def phase_parts(channels):
    cell_index = jnp.arange(CHANNELS, dtype=jnp.int32)
    phase_turns = channels[:, None] * cell_index[None, :] % CHANNELS
    phase_angle = phase_turns.astype(jnp.float32) * (2.0 * math.pi / CHANNELS)
    scale_factor = 1.0 / math.sqrt(CHANNELS)
    return (jnp.cos(phase_angle) * scale_factor, jnp.sin(phase_angle) * scale_factor)

def channel_table(channels):
    cosine, sine_part = phase_parts(channels)
    forward = jnp.stack([jnp.stack([cosine, sine_part], 1), jnp.stack([-sine_part, cosine], 1)], 0)
    return forward.astype(jnp.bfloat16)

def lag_table(channels):
    cosine, sine_part = phase_parts(channels)
    cosine = cosine.T
    sine_part = sine_part.T
    backward = jnp.stack([jnp.stack([cosine, -sine_part], 2), jnp.stack([sine_part, cosine], 2)], 0)
    return backward.astype(jnp.bfloat16)

def filter_bank(segment, window):
    framed = segment.reshape(segment.shape[:-1] + (SPECTRA + TAPS - 1, CHANNELS))
    total = jnp.zeros(segment.shape[:-1] + (SPECTRA, CHANNELS), jnp.float32)
    for tap_index in range(TAPS):
        total = total + framed[..., tap_index:tap_index + SPECTRA, :].astype(jnp.float32) * window[tap_index]
    return total.astype(jnp.bfloat16)

def reference(voltages, delay_table, channel_map, row_assign):
    window = prototype().astype(jnp.float32)
    natural = jnp.arange(CHANNELS, dtype=jnp.int32)
    forward = channel_table(natural)
    span = (SPECTRA + TAPS - 1) * CHANNELS

    def channelize(pair):
        station_volts, delay = pair
        segment = lax.dynamic_slice_in_dim(station_volts, delay.astype(jnp.int32), span, 2)
        filtered = filter_bank(segment, window)
        spectra = jnp.einsum('qkpc,apsc->aqks', forward.astype(jnp.float32), filtered.astype(jnp.float32))
        return spectra.astype(jnp.bfloat16)
    spectra = lax.map(channelize, (voltages, delay_table))
    by_channel = jnp.moveaxis(spectra, 3, 0)

    def correlate(channel_block):
        real_part = channel_block[:, :, 0].reshape(INPUTS, SPECTRA)
        imag_part = channel_block[:, :, 1].reshape(INPUTS, SPECTRA)
        vis_real = (jnp.dot(real_part, real_part.T, preferred_element_type=jnp.float32) + jnp.dot(imag_part, imag_part.T, preferred_element_type=jnp.float32)) / SPECTRA
        vis_imag = (jnp.dot(imag_part, real_part.T, preferred_element_type=jnp.float32) - jnp.dot(real_part, imag_part.T, preferred_element_type=jnp.float32)) / SPECTRA
        return (jnp.stack([vis_real, vis_imag]).astype(jnp.bfloat16), jnp.diagonal(vis_real))
    visibility, autos = lax.map(correlate, by_channel)
    bandpass = jnp.take(autos, channel_map, axis=0)
    backward = lag_table(natural).astype(jnp.float32)
    lag_position = jnp.where(natural < CHANNELS // 2, natural, natural - CHANNELS).astype(jnp.float32) / (CHANNELS // 2)

    def transform(block_id):
        rows = lax.dynamic_slice_in_dim(visibility, (block_id * ROWB).astype(jnp.int32), ROWB, 2)
        lag = jnp.einsum('qlkp,kprj->qlrj', backward, rows.astype(jnp.float32))
        power = lag[0] * lag[0] + lag[1] * lag[1]
        delay = lax.optimization_barrier(jnp.sum(power * lag_position[:, None, None], 0)) / (lax.optimization_barrier(jnp.sum(power, 0)) + 1e-06)
        return (lag.astype(jnp.bfloat16), delay)
    lags, delays = lax.map(transform, row_assign)
    return (bandpass, lags, delays)
```

```python
import math

import jax
import jax.numpy as jnp
from jax import lax
from jax.sharding import PartitionSpec as P

CHANNELS = 256
TAPS = 8
SPECTRA = 512
AXES = ("stn", "pol")


def prototype_at(sample_index):
    tap_total = TAPS * CHANNELS
    taper_values = 0.5 - 0.5 * jnp.cos(2.0 * math.pi * (sample_index + 0.5) / tap_total)
    offset = (sample_index - (tap_total - 1) / 2.0) / CHANNELS
    return jnp.sin(math.pi * offset) / (math.pi * offset) * taper_values


def shifted_windows(delays):
    tap_total = TAPS * CHANNELS
    base = prototype_at(jnp.arange(tap_total, dtype=jnp.float32))
    scale = jnp.sqrt(CHANNELS / jnp.sum(base * base))
    index = jnp.arange((TAPS + 1) * CHANNELS, dtype=jnp.int32)[None, :] - delays[:, None]
    valid = (index >= 0) & (index < tap_total)
    values = prototype_at(index.astype(jnp.float32)) * scale
    return jnp.where(valid, values, 0.0).reshape(-1, TAPS + 1, CHANNELS)


def phase_parts(channels):
    cell_index = jnp.arange(CHANNELS, dtype=jnp.int32)
    phase_turns = channels[:, None] * cell_index[None, :] % CHANNELS
    phase_angle = phase_turns.astype(jnp.float32) * (2.0 * math.pi / CHANNELS)
    scale_factor = 1.0 / math.sqrt(CHANNELS)
    return (jnp.cos(phase_angle) * scale_factor, jnp.sin(phase_angle) * scale_factor)


def per_device(voltages, delay_table, channel_map, row_assign):
    owner_count = lax.axis_size("stn") * lax.axis_size("pol")
    stn_count = lax.axis_size("stn")
    pol_count = lax.axis_size("pol")
    local = CHANNELS // owner_count
    stations = voltages.shape[0]
    cosine, sine = phase_parts(channel_map)
    cosine = cosine.astype(jnp.bfloat16)
    sine = sine.astype(jnp.bfloat16)
    position = jnp.arange(CHANNELS, dtype=jnp.int32)

    forward = jnp.stack([jnp.stack([cosine, sine], 1), jnp.stack([-sine, cosine], 1)], 0)
    source = (position[None, :] - delay_table[:, None]) % CHANNELS
    roll = (position[None, :, None] == source[:, None, :]).astype(jnp.bfloat16)
    rolled = jnp.einsum(
        "qkpc,acd->aqkpd", forward, roll, preferred_element_type=jnp.float32
    ).astype(jnp.bfloat16)

    window = shifted_windows(delay_table)
    frames = SPECTRA + TAPS
    pad = frames * CHANNELS - voltages.shape[-1]
    framed = jnp.pad(voltages[:, 0], ((0, 0), (0, 0), (0, pad)))
    framed = framed.reshape(stations, 2, frames, CHANNELS)
    total = jnp.zeros((stations, 2, SPECTRA, CHANNELS), jnp.float32)
    for tap in range(TAPS + 1):
        total = total + framed[:, :, tap : tap + SPECTRA].astype(jnp.float32) * window[
            :, None, tap, None, :
        ]
    filtered = total.astype(jnp.bfloat16)

    spectra = jnp.einsum(
        "aqkpc,apsc->aqks", rolled, filtered, preferred_element_type=jnp.float32
    ).astype(jnp.bfloat16)
    outgoing = spectra.reshape(stations, 2, owner_count, local, SPECTRA).transpose(2, 3, 1, 0, 4)
    turned = lax.all_to_all(outgoing, AXES, split_axis=0, concat_axis=0, tiled=True)
    turned = turned.reshape(stn_count, pol_count, local, 2, stations, SPECTRA)
    inputs = owner_count * stations
    block = turned.transpose(2, 3, 0, 4, 1, 5).reshape(local, 2 * inputs, SPECTRA)

    gram = jnp.einsum("kis,kjs->kij", block, block, preferred_element_type=jnp.float32)
    vis_re = (gram[:, :inputs, :inputs] + gram[:, inputs:, inputs:]) / SPECTRA
    vis_im = (gram[:, inputs:, :inputs] - gram[:, :inputs, inputs:]) / SPECTRA
    wide = block.astype(jnp.float32)
    energy = jnp.sum(wide * wide, -1)
    bandpass = (energy[:, :inputs] + energy[:, inputs:]) / SPECTRA

    visibility = jnp.stack([vis_re, vis_im], 1).astype(jnp.bfloat16)
    rows = inputs // owner_count
    blocked = visibility.reshape(local, 2, owner_count, rows, inputs)
    arranged = jnp.take(blocked, row_assign, axis=2).transpose(2, 0, 1, 3, 4)
    gathered = lax.all_to_all(arranged, AXES, split_axis=0, concat_axis=0, tiled=True)
    gathered = gathered.reshape(CHANNELS, 2, rows * inputs)

    backward = jnp.stack(
        [jnp.stack([cosine.T, -sine.T], 2), jnp.stack([sine.T, cosine.T], 2)], 0
    )
    lag = jnp.einsum("qlkp,kpm->qlm", backward, gathered, preferred_element_type=jnp.float32)
    power = lag[0] * lag[0] + lag[1] * lag[1]
    lag_position = jnp.where(position < CHANNELS // 2, position, position - CHANNELS).astype(
        jnp.float32
    ) / (CHANNELS // 2)
    delay = jnp.sum(power * lag_position[:, None], 0) / (jnp.sum(power, 0) + 1e-06)
    lags = lag.astype(jnp.bfloat16).reshape(1, 2, CHANNELS, rows, inputs)
    return (bandpass, lags, delay.reshape(1, rows, inputs))


def solution(mesh):
    in_specs = (P("stn", "pol", None, None), P("stn"), P(), P())
    out_specs = (
        P(AXES, None),
        P(AXES, None, None, None, None),
        P(AXES, None, None),
    )
    return jax.shard_map(
        per_device, mesh=mesh, in_specs=in_specs, out_specs=out_specs, check_vma=False
    )
```

```python
import math

import jax
import jax.numpy as jnp
from jax import lax
from jax.sharding import PartitionSpec as P

CHANNELS = 256
TAPS = 8
SPECTRA = 512
AXES = ("stn", "pol")
CHUNKS = (256, 256)


def prototype_at(sample_index):
    tap_total = TAPS * CHANNELS
    taper_values = 0.5 - 0.5 * jnp.cos(2.0 * math.pi * (sample_index + 0.5) / tap_total)
    offset = (sample_index - (tap_total - 1) / 2.0) / CHANNELS
    return jnp.sin(math.pi * offset) / (math.pi * offset) * taper_values


def shifted_windows(delays):
    tap_total = TAPS * CHANNELS
    base = prototype_at(jnp.arange(tap_total, dtype=jnp.float32))
    scale = jnp.sqrt(CHANNELS / jnp.sum(base * base))
    index = jnp.arange((TAPS + 1) * CHANNELS, dtype=jnp.int32)[None, :] - delays[:, None]
    valid = (index >= 0) & (index < tap_total)
    values = prototype_at(index.astype(jnp.float32)) * scale
    return jnp.where(valid, values, 0.0).reshape(-1, TAPS + 1, CHANNELS)


def folded_sine(quarter):
    x = quarter * (2.0 * math.pi / CHANNELS)
    y = x * x
    series = -1.0 / 39916800.0
    for factor in (1.0 / 362880.0, -1.0 / 5040.0, 1.0 / 120.0, -1.0 / 6.0, 1.0):
        series = series * y + factor
    return x * series / math.sqrt(CHANNELS)


def phase_parts(channels):
    cell_index = jnp.arange(CHANNELS, dtype=jnp.int32)
    turns = channels[:, None] * cell_index[None, :] % CHANNELS
    half, quarter = CHANNELS // 2, CHANNELS // 4
    cosine = jnp.abs(turns - half) - quarter
    sine = jnp.abs((turns - quarter) % CHANNELS - half) - quarter
    return (folded_sine(cosine.astype(jnp.float32)), folded_sine(sine.astype(jnp.float32)))


def per_device(voltages, delay_table, channel_map, row_assign):
    owner_count = lax.axis_size("stn") * lax.axis_size("pol")
    stn_count = lax.axis_size("stn")
    pol_count = lax.axis_size("pol")
    local = CHANNELS // owner_count
    stations = voltages.shape[0]
    cosine, sine = phase_parts(channel_map)
    cosine = cosine.astype(jnp.bfloat16)
    sine = sine.astype(jnp.bfloat16)
    position = jnp.arange(CHANNELS, dtype=jnp.int32)

    forward = jnp.stack([jnp.stack([cosine, sine], 1), jnp.stack([-sine, cosine], 1)], 0)
    source = (position[None, :] - delay_table[:, None]) % CHANNELS
    roll = (position[None, :, None] == source[:, None, :]).astype(jnp.bfloat16)
    rolled = jnp.einsum(
        "qkpc,acd->aqkpd", forward, roll, preferred_element_type=jnp.float32
    ).astype(jnp.bfloat16)

    window = shifted_windows(delay_table)
    inputs = owner_count * stations

    def exchange(start, count):
        first = start * CHANNELS
        last = min((start + count + TAPS) * CHANNELS, voltages.shape[-1])
        framed = voltages[:, 0, :, first:last]
        pad = (count + TAPS) * CHANNELS - (last - first)
        framed = jnp.pad(framed, ((0, 0), (0, 0), (0, pad)))
        framed = framed.reshape(stations, 2, count + TAPS, CHANNELS)
        total = jnp.zeros((stations, 2, count, CHANNELS), jnp.float32)
        for tap in range(TAPS + 1):
            total = total + framed[:, :, tap : tap + count].astype(jnp.float32) * window[
                :, None, tap, None, :
            ]
        spectra = jnp.einsum(
            "aqkpc,apsc->aqks",
            rolled,
            total.astype(jnp.bfloat16),
            preferred_element_type=jnp.float32,
        ).astype(jnp.bfloat16)
        outgoing = spectra.reshape(stations, 2, owner_count, local, count)
        outgoing = outgoing.transpose(2, 3, 1, 0, 4)
        return lax.all_to_all(outgoing, AXES, split_axis=0, concat_axis=0, tiled=True)

    gram = jnp.zeros((local, 2 * inputs, 2 * inputs), jnp.float32)
    energy = jnp.zeros((local, 2 * inputs), jnp.float32)
    start = 0
    for count in CHUNKS:
        turned = exchange(start, count)
        start += count
        turned = turned.reshape(stn_count, pol_count, local, 2, stations, count)
        block = turned.transpose(2, 3, 0, 4, 1, 5).reshape(local, 2 * inputs, count)
        gram = gram + jnp.einsum("kis,kjs->kij", block, block, preferred_element_type=jnp.float32)
        wide = block.astype(jnp.float32)
        energy = energy + jnp.sum(wide * wide, -1)
    vis_re = (gram[:, :inputs, :inputs] + gram[:, inputs:, inputs:]) / SPECTRA
    vis_im = (gram[:, inputs:, :inputs] - gram[:, :inputs, inputs:]) / SPECTRA
    bandpass = (energy[:, :inputs] + energy[:, inputs:]) / SPECTRA

    visibility = jnp.stack([vis_re, vis_im], 1).astype(jnp.bfloat16)
    rows = inputs // owner_count
    blocked = visibility.reshape(local, 2, owner_count, rows, inputs)
    arranged = jnp.take(blocked, row_assign, axis=2).transpose(2, 0, 1, 3, 4)
    gathered = lax.all_to_all(arranged, AXES, split_axis=0, concat_axis=0, tiled=True)
    gathered = gathered.reshape(CHANNELS, 2, rows * inputs)

    backward = jnp.stack(
        [jnp.stack([cosine.T, -sine.T], 2), jnp.stack([sine.T, cosine.T], 2)], 0
    )
    lag = jnp.einsum("qlkp,kpm->qlm", backward, gathered, preferred_element_type=jnp.float32)
    power = lag[0] * lag[0] + lag[1] * lag[1]
    lag_position = jnp.where(position < CHANNELS // 2, position, position - CHANNELS).astype(
        jnp.float32
    ) / (CHANNELS // 2)
    delay = jnp.sum(power * lag_position[:, None], 0) / (jnp.sum(power, 0) + 1e-06)
    lags = lag.astype(jnp.bfloat16).reshape(1, 2, CHANNELS, rows, inputs)
    return (bandpass, lags, delay.reshape(1, rows, inputs))


def solution(mesh):
    in_specs = (P("stn", "pol", None, None), P("stn"), P(), P())
    out_specs = (
        P(AXES, None),
        P(AXES, None, None, None, None),
        P(AXES, None, None),
    )
    return jax.shard_map(
        per_device, mesh=mesh, in_specs=in_specs, out_specs=out_specs, check_vma=False
    )
```

```python
import math

import jax
import jax.numpy as jnp
from jax import lax
from jax.experimental import pallas as pl
from jax.experimental.pallas import tpu as pltpu
from jax.sharding import PartitionSpec as P

CHANNELS = 256
TAPS = 8
SPECTRA = 512
AXES = ("stn", "pol")
CHUNKS = (256, 256)


def prototype_at(sample_index):
    tap_total = TAPS * CHANNELS
    taper_values = 0.5 - 0.5 * jnp.cos(2.0 * math.pi * (sample_index + 0.5) / tap_total)
    offset = (sample_index - (tap_total - 1) / 2.0) / CHANNELS
    return jnp.sin(math.pi * offset) / (math.pi * offset) * taper_values


def shifted_windows(delays):
    tap_total = TAPS * CHANNELS
    base = prototype_at(jnp.arange(tap_total, dtype=jnp.float32))
    scale = jnp.sqrt(CHANNELS / jnp.sum(base * base))
    index = jnp.arange((TAPS + 1) * CHANNELS, dtype=jnp.int32)[None, :] - delays[:, None]
    valid = (index >= 0) & (index < tap_total)
    values = prototype_at(index.astype(jnp.float32)) * scale
    return jnp.where(valid, values, 0.0).reshape(-1, TAPS + 1, CHANNELS)


def folded_sine(quarter):
    x = quarter * (2.0 * math.pi / CHANNELS)
    y = x * x
    series = -1.0 / 39916800.0
    for factor in (1.0 / 362880.0, -1.0 / 5040.0, 1.0 / 120.0, -1.0 / 6.0, 1.0):
        series = series * y + factor
    return x * series / math.sqrt(CHANNELS)


def phase_parts(channels):
    cell_index = jnp.arange(CHANNELS, dtype=jnp.int32)
    turns = channels[:, None] * cell_index[None, :] % CHANNELS
    half, quarter = CHANNELS // 2, CHANNELS // 4
    cosine = jnp.abs(turns - half) - quarter
    sine = jnp.abs((turns - quarter) % CHANNELS - half) - quarter
    return (folded_sine(cosine.astype(jnp.float32)), folded_sine(sine.astype(jnp.float32)))


def row_table(channels):
    rows = lax.broadcasted_iota(jnp.int32, (2 * CHANNELS, 2 * CHANNELS), 0)
    cells = lax.broadcasted_iota(jnp.int32, (2 * CHANNELS, 2 * CHANNELS), 1)
    quarter = CHANNELS // 4
    turns = jnp.repeat(channels, 2)[:, None] * (cells % CHANNELS)
    turns = (turns + quarter * (rows % 2 - cells // CHANNELS)) % CHANNELS
    folded = jnp.abs(turns - CHANNELS // 2) - quarter
    return folded_sine(folded.astype(jnp.float32)).astype(jnp.bfloat16)


def each(count, body):
    def step(index, carry):
        body(index)
        return carry

    lax.fori_loop(0, count, step, 0)


def exchange_kernel(
    filtered, framed, window, table, shift, regroup, gram, stage, send, recv, block, send_sem, recv_sem
):
    pol_count = lax.axis_size("pol")
    owners = lax.axis_size("stn") * pol_count
    me = lax.axis_index("stn") * pol_count + lax.axis_index("pol")
    stations = filtered.shape[0]
    count = filtered.shape[2]

    def place(index):
        return (index // pol_count, index % pol_count)

    barrier = pltpu.get_barrier_semaphore()

    def greet(offset):
        pl.semaphore_signal(
            barrier,
            inc=1,
            device_id=place((me + 1 + offset) % owners),
            device_id_type=pl.DeviceIdType.MESH,
        )

    each(owners - 1, greet)

    def remote(half, source, target):
        return pltpu.make_async_remote_copy(
            src_ref=send.at[half, target],
            dst_ref=recv.at[half, source],
            send_sem=send_sem.at[half, target],
            recv_sem=recv_sem.at[half, source],
            device_id=place(target),
            device_id_type=pl.DeviceIdType.MESH,
        )

    def own(half):
        return pltpu.make_async_copy(
            send.at[half, me], recv.at[half, me], recv_sem.at[half, me]
        )

    def turn(rows, moves):
        return jnp.dot(rows, moves, preferred_element_type=jnp.float32).astype(jnp.bfloat16)

    def transform(half, values):
        def station(a):
            product = lax.dot_general(
                turn(table[:, :CHANNELS], shift[a]),
                values[a, 0],
                (((1,), (1,)), ((), ())),
                preferred_element_type=jnp.float32,
            ) + lax.dot_general(
                turn(table[:, CHANNELS:], shift[a]),
                values[a, 1],
                (((1,), (1,)), ((), ())),
                preferred_element_type=jnp.float32,
            )
            send[half, :, a] = product.astype(jnp.bfloat16).reshape(owners, -1, count)

        each(stations, station)

    def deliver(half):
        own(half).start()

        def start(step):
            offset = step // 4 + (owners // 4) * ((step + 2) % 4)

            @pl.when(offset != 0)
            def _():
                remote(half, me, (me + offset) % owners).start()

        each(owners, start)

    def filter_rest():
        def part(index):
            a = index // 2
            p = index % 2
            total = jnp.zeros((count, CHANNELS), jnp.float32)
            wide = framed[a, p].astype(jnp.float32)
            for tap in range(TAPS + 1):
                total = total + wide[tap : tap + count] * window[a, tap : tap + 1]
            stage[a, p] = total.astype(jnp.bfloat16)

        each(stations * 2, part)

    def correlate(half):
        group = 256 // (stations * block.shape[0])

        own(half).wait()

        def arrive(offset):
            remote(half, (me + 1 + offset) % owners, me).wait_recv()

        each(owners - 1, arrive)

        def gather(g):
            rows = recv[half, pl.ds(g * group, group)].reshape(256, count)
            moved = jnp.dot(regroup[...], rows, preferred_element_type=jnp.float32)
            width = group * stations
            block[:, pl.ds(pl.multiple_of(g * width, width), width)] = moved.astype(
                jnp.bfloat16
            ).reshape(-1, width, count)

        each(owners // group, gather)

        def channel(k):
            rows = block[pl.ds(2 * k, 2)].reshape(-1, count)
            product = lax.dot_general(
                rows, rows, (((1,), (1,)), ((), ())), preferred_element_type=jnp.float32
            )
            if half == 0:
                gram[k] = product
            else:
                gram[k] = gram[k] + product

        each(gram.shape[0], channel)

    transform(0, filtered)
    pl.semaphore_wait(barrier, owners - 1)
    deliver(0)
    filter_rest()
    transform(1, stage)
    deliver(1)
    correlate(0)
    correlate(1)

    def sent(offset):
        target = (me + 1 + offset) % owners
        for half in range(2):
            pltpu.make_async_remote_copy(
                src_ref=send.at[half, target],
                dst_ref=recv.at[half, me],
                send_sem=send_sem.at[half, target],
                recv_sem=recv_sem.at[half, me],
                device_id=place(target),
                device_id_type=pl.DeviceIdType.MESH,
            ).wait_send()

    each(owners - 1, sent)


def kernel_gram(filtered, framed, window, table, shift, owners, local):
    stations = filtered.shape[0]
    count = filtered.shape[2]
    rows = 2 * local
    inputs = owners * stations
    group = 256 // (stations * rows)
    index = jnp.arange(256, dtype=jnp.int32)
    r, il = index // (group * stations), index % (group * stations)
    stn, rest = il // (2 * stations), il % (2 * stations)
    source = ((stn * 2 + rest % 2) * stations + rest // 2) * rows + r
    regroup = (index[None, :] == source[:, None]).astype(jnp.bfloat16)
    vmem = pl.BlockSpec(memory_space=pltpu.VMEM)
    return pl.pallas_call(
        exchange_kernel,
        out_shape=jax.ShapeDtypeStruct((local, 2 * inputs, 2 * inputs), jnp.float32),
        in_specs=[vmem] * 6,
        out_specs=vmem,
        scratch_shapes=[
            pltpu.VMEM((stations, 2, count, CHANNELS), jnp.bfloat16),
            pltpu.VMEM((2, owners, stations, rows, count), jnp.bfloat16),
            pltpu.VMEM((2, owners, stations, rows, count), jnp.bfloat16),
            pltpu.VMEM((rows, inputs, count), jnp.bfloat16),
            pltpu.SemaphoreType.DMA((2, owners)),
            pltpu.SemaphoreType.DMA((2, owners)),
        ],
        compiler_params=pltpu.CompilerParams(
            collective_id=0, has_side_effects=True, vmem_limit_bytes=48 * 1024 * 1024
        ),
    )(filtered, framed, window, table, shift, regroup)


def per_device(voltages, delay_table, channel_map, row_assign):
    owner_count = lax.axis_size("stn") * lax.axis_size("pol")
    stn_count = lax.axis_size("stn")
    pol_count = lax.axis_size("pol")
    local = CHANNELS // owner_count
    stations = voltages.shape[0]
    cosine, sine = phase_parts(channel_map)
    cosine = cosine.astype(jnp.bfloat16)
    sine = sine.astype(jnp.bfloat16)
    position = jnp.arange(CHANNELS, dtype=jnp.int32)

    forward = jnp.stack([jnp.stack([cosine, sine], 1), jnp.stack([-sine, cosine], 1)], 0)
    source = (position[None, :] - delay_table[:, None]) % CHANNELS
    roll = (position[None, :, None] == source[:, None, :]).astype(jnp.bfloat16)
    rolled = jnp.einsum(
        "qkpc,acd->aqkpd", forward, roll, preferred_element_type=jnp.float32
    ).astype(jnp.bfloat16)

    window = shifted_windows(delay_table)
    inputs = owner_count * stations

    def frame(start, count):
        first = start * CHANNELS
        last = min((start + count + TAPS) * CHANNELS, voltages.shape[-1])
        framed = voltages[:, 0, :, first:last]
        pad = (count + TAPS) * CHANNELS - (last - first)
        framed = jnp.pad(framed, ((0, 0), (0, 0), (0, pad)))
        return framed.reshape(stations, 2, count + TAPS, CHANNELS)

    def filter_frames(framed, count):
        total = jnp.zeros((stations, 2, count, CHANNELS), jnp.float32)
        for tap in range(TAPS + 1):
            total = total + framed[:, :, tap : tap + count].astype(jnp.float32) * window[
                :, None, tap, None, :
            ]
        return total.astype(jnp.bfloat16)

    def exchange(start, count):
        filtered = filter_frames(frame(start, count), count)
        spectra = jnp.einsum(
            "aqkpc,apsc->aqks",
            rolled,
            filtered,
            preferred_element_type=jnp.float32,
        ).astype(jnp.bfloat16)
        outgoing = spectra.reshape(stations, 2, owner_count, local, count)
        outgoing = outgoing.transpose(2, 3, 1, 0, 4)
        return lax.all_to_all(outgoing, AXES, split_axis=0, concat_axis=0, tiled=True)

    if local * stations * 2 == 64 and pol_count == 2:
        count = SPECTRA // 2
        table = row_table(channel_map)
        gram = kernel_gram(
            filter_frames(frame(0, count), count),
            frame(count, count),
            window,
            table,
            roll,
            owner_count,
            local,
        )
        same = jnp.arange(2 * inputs)[:, None] == jnp.arange(2 * inputs)[None, :]
        energy = jnp.sum(jnp.where(same, gram, 0.0), -1)
    else:
        gram = jnp.zeros((local, 2 * inputs, 2 * inputs), jnp.float32)
        energy = jnp.zeros((local, 2 * inputs), jnp.float32)
        start = 0
        for count in CHUNKS:
            turned = exchange(start, count)
            start += count
            turned = turned.reshape(stn_count, pol_count, local, 2, stations, count)
            block = turned.transpose(2, 3, 0, 4, 1, 5).reshape(local, 2 * inputs, count)
            gram = gram + jnp.einsum("kis,kjs->kij", block, block, preferred_element_type=jnp.float32)
            wide = block.astype(jnp.float32)
            energy = energy + jnp.sum(wide * wide, -1)
    vis_re = (gram[:, :inputs, :inputs] + gram[:, inputs:, inputs:]) / SPECTRA
    vis_im = (gram[:, inputs:, :inputs] - gram[:, :inputs, inputs:]) / SPECTRA
    bandpass = (energy[:, :inputs] + energy[:, inputs:]) / SPECTRA

    visibility = jnp.stack([vis_re, vis_im], 1).astype(jnp.bfloat16)
    rows = inputs // owner_count
    blocked = visibility.reshape(local, 2, owner_count, rows, inputs)
    arranged = jnp.take(blocked, row_assign, axis=2).transpose(2, 0, 1, 3, 4)
    gathered = lax.all_to_all(arranged, AXES, split_axis=0, concat_axis=0, tiled=True)
    gathered = gathered.reshape(CHANNELS, 2, rows * inputs)

    backward = jnp.stack(
        [jnp.stack([cosine.T, -sine.T], 2), jnp.stack([sine.T, cosine.T], 2)], 0
    )
    lag = jnp.einsum("qlkp,kpm->qlm", backward, gathered, preferred_element_type=jnp.float32)
    power = lag[0] * lag[0] + lag[1] * lag[1]
    lag_position = jnp.where(position < CHANNELS // 2, position, position - CHANNELS).astype(
        jnp.float32
    ) / (CHANNELS // 2)
    delay = jnp.sum(power * lag_position[:, None], 0) / (jnp.sum(power, 0) + 1e-06)
    lags = lag.astype(jnp.bfloat16).reshape(1, 2, CHANNELS, rows, inputs)
    return (bandpass, lags, delay.reshape(1, rows, inputs))


def solution(mesh):
    in_specs = (P("stn", "pol", None, None), P("stn"), P(), P())
    out_specs = (
        P(AXES, None),
        P(AXES, None, None, None, None),
        P(AXES, None, None),
    )
    return jax.shard_map(
        per_device, mesh=mesh, in_specs=in_specs, out_specs=out_specs, check_vma=False
    )
```
